512 devices in a mesh: blk: 4 (over x_lo, core), grp: 128 (over x_hi, y, z).
Axes of the slice: x: 4 (x_hi: 2, x_lo: 2; x = x_hi * 2 + x_lo), y: 4, z: 16, core: 2. Of those that a mesh axis runs over, the one named last changes fastest.
Arguments:
- text: bfloat16 [512, 512], P(('blk', 'grp')), may hold values from -20 to 20
- keys: bfloat16 [512, 196, 512], P(('blk', 'grp')), may hold values from -400 to 400
- values: bfloat16 [512, 196, 512], P(('blk', 'grp')), may hold values from -5 to 5
- pair_image: int32 [512], replicated, may hold values from 0 to 511, each once
Outputs:
- caption_loss: float32 [512], P(('blk', 'grp'))
- grad_text: float32 [512, 512], P(('blk', 'grp'))
- grad_keys: float32 [512, 196, 512], P(('blk', 'grp'))
- grad_values: float32 [512, 196, 512], P(('blk', 'grp'))
The draws below stay inside these ranges and needn't reach their ends.
All inputs are finite; a program needn't handle non-finite values.
Results may differ from the reference program's by a relative error of at most 0.008.
Values may be sent and summed in bfloat16 or wider, within the bound.
No kernel may reach another device: no remote copies, remote signals or barrier semaphores. Data moves between devices by JAX's collectives and lax.ppermute only.
A program may use at most 64 MiB of HBM per device.

```python
import jax
import jax.numpy as jnp
from jax import lax

D = 512
HEADS = 8
PATCHES = 196
IMAGES = 512
CAPTIONS = 512


def shared_text(key):
    base = jax.random.normal(jax.random.fold_in(key, 11), (CAPTIONS, D), jnp.float32)
    base = jnp.clip(base, -4.0, 4.0)
    return base


def draw_text(key, part):
    return shared_text(key).astype(jnp.bfloat16)


def draw_keys(key, part):
    base = jax.random.normal(jax.random.fold_in(key, 13), (IMAGES, PATCHES, D), jnp.float32)
    base = jnp.clip(base, -4.0, 4.0)
    return base.astype(jnp.bfloat16)


def level_of(stream_key, extent, cuts, low, largest):
    def one(dim, blocks):
        steps = jax.random.uniform(jax.random.fold_in(jax.random.fold_in(stream_key, 6), dim), (blocks,), jnp.float32, low / len(cuts), largest / len(cuts))
        return jnp.repeat(jnp.exp(steps), extent[dim] // blocks).reshape((-1,) + (1,) * (len(extent) - dim - 1))

    loudness = one(*cuts[0])
    for cut in cuts[1:]:
        loudness = loudness * one(*cut)
    return loudness


def bell_draw(rng, extent, scale, limit, cuts=(), kind=jnp.bfloat16):
    entries = jax.random.normal(rng, extent, jnp.float32) * scale
    if len(cuts) > 0:
        entries = level_of(rng, extent, cuts, -0.22, 0.18) * entries
    return jnp.clip(entries, min=-limit, max=limit).astype(kind)


def setup_inputs(seed: int = 0) -> dict:
    arg_keys = jax.random.split(jax.random.key(seed), 5)
    text = draw_text(jax.random.fold_in(arg_keys[4], 71), 0)
    keys = draw_keys(jax.random.fold_in(arg_keys[4], 71), 0)
    values = bell_draw(arg_keys[2], (IMAGES, PATCHES, D), 1.0, 5.0, ((0, 512),))
    pair_image = jax.random.permutation(arg_keys[3], IMAGES).astype(jnp.int32)
    return dict(text=text, keys=keys, values=values, pair_image=pair_image)


EPS = 1e-06
LOGIT_SCALE = 10.0
LOGIT_BIAS = -1.0

def image_terms(text, normed, tnorm, pairs, image_id, keys_one, values_one):
    count = text.shape[0]
    width = text.shape[1]
    depth = width // HEADS
    queries = text.astype(jnp.float32).reshape(count, HEADS, depth)
    patch_keys = keys_one.astype(jnp.float32).reshape(-1, HEADS, depth)
    patch_values = values_one.astype(jnp.float32).reshape(-1, HEADS, depth)
    hi = lax.Precision.HIGHEST
    scores = jnp.einsum('chd,phd->chp', queries, patch_keys, precision=hi) * depth ** (-0.5)
    weights = jax.nn.softmax(scores, axis=-1)
    attn = weights.astype(jnp.bfloat16)
    attn_wide = attn.astype(jnp.float32)
    pooled = jnp.einsum('chp,phd->chd', attn_wide, patch_values, precision=hi).reshape(count, width)
    pnorm = lax.rsqrt(lax.optimization_barrier(jnp.mean(pooled * pooled, -1, keepdims=True)) + EPS)
    unit = pooled * pnorm
    cosine = lax.optimization_barrier(jnp.mean(unit * normed, -1))
    logit = LOGIT_SCALE * cosine + LOGIT_BIAS
    label = jnp.where(pairs == image_id, 1.0, -1.0).astype(jnp.float32)
    loss = jax.nn.softplus(-label * logit)
    slope = -label * jax.nn.sigmoid(-label * logit)
    dcos = LOGIT_SCALE / width * slope[:, None]
    dunit = dcos * normed
    dnormed = dcos * unit
    dpool = pnorm * (dunit - unit * lax.optimization_barrier(jnp.mean(dunit * unit, -1, keepdims=True)))
    dout = dpool.astype(jnp.bfloat16).astype(jnp.float32).reshape(count, HEADS, depth)
    dattn = jnp.einsum('chd,phd->chp', dout, patch_values, precision=hi)
    grad_v = jnp.einsum('chp,chd->phd', attn_wide, dout, precision=hi).reshape(-1, width)
    dscore = weights * (dattn - lax.optimization_barrier(jnp.sum(weights * dattn, -1, keepdims=True))) * depth ** (-0.5)
    dscore = dscore.astype(jnp.bfloat16).astype(jnp.float32)
    grad_q = jnp.einsum('chp,phd->chd', dscore, patch_keys, precision=hi).reshape(count, width)
    grad_k = jnp.einsum('chp,chd->phd', dscore, queries, precision=hi).reshape(-1, width)
    grad_x = grad_q + tnorm * (dnormed - normed * lax.optimization_barrier(jnp.mean(dnormed * normed, -1, keepdims=True)))
    return (loss, grad_x, grad_k, grad_v)

def reference(text, keys, values, pair_image):
    count = text.shape[0]
    text_wide = text.astype(jnp.float32)
    tnorm = lax.rsqrt(lax.optimization_barrier(jnp.mean(text_wide * text_wide, -1, keepdims=True)) + EPS)
    normed = text_wide * tnorm
    image_ids = jnp.arange(IMAGES, dtype=jnp.int32)

    def one_image(carry, item):
        keys_one, values_one, image_id = item
        loss, grad_x, grad_k, grad_v = image_terms(text, normed, tnorm, pair_image, image_id, keys_one, values_one)
        return ((carry[0] + loss, carry[1] + grad_x), (grad_k, grad_v))
    start = (jnp.zeros((count,), jnp.float32), jnp.zeros((count, D), jnp.float32))
    (loss_sum, grad_text), (grad_keys, grad_values) = lax.scan(one_image, start, (keys, values, image_ids))
    return (loss_sum / IMAGES, grad_text, grad_keys, grad_values)
```

```python
import jax
import jax.numpy as jnp
from jax import lax
from jax.sharding import Mesh
from jax.sharding import PartitionSpec as P

HEADS = 8
PLANE = ("blk", "row")
LINE = ("line",)


EPS = 1e-06
LOGIT_SCALE = 10.0
LOGIT_BIAS = -1.0


def gathered(shard, axes):
    held = lax.axis_size(axes)
    spread = jnp.broadcast_to(shard[None], (held, *shard.shape))
    return lax.all_to_all(spread, axes, 0, 0, tiled=True).reshape(-1, *shard.shape[1:])


def scattered_sum(rows, axes):
    held = lax.axis_size(axes)
    parts = rows.reshape(held, -1, rows.shape[1])
    arrived = lax.all_to_all(parts, axes, 0, 0, tiled=True)
    return jnp.sum(arrived.astype(jnp.float32), axis=0)


def image_terms(block_text, normed, tnorm, pairs, image_id, keys_one, values_one):
    count = block_text.shape[0]
    width = block_text.shape[1]
    depth = width // HEADS
    queries = block_text.reshape(count, HEADS, depth)
    patch_keys = keys_one.reshape(-1, HEADS, depth)
    patch_values = values_one.reshape(-1, HEADS, depth)
    scores = jnp.einsum(
        "chd,phd->chp", queries, patch_keys, preferred_element_type=jnp.float32
    ) * depth ** (-0.5)
    weights = jax.nn.softmax(scores, axis=-1)
    attn = weights.astype(jnp.bfloat16)
    pooled = jnp.einsum(
        "chp,phd->chd", attn, patch_values, preferred_element_type=jnp.float32
    ).reshape(count, width)
    pnorm = lax.rsqrt(jnp.mean(pooled * pooled, -1, keepdims=True) + EPS)
    unit = pooled * pnorm
    cosine = jnp.mean(unit * normed, -1)
    logit = LOGIT_SCALE * cosine + LOGIT_BIAS
    label = jnp.where(pairs == image_id, 1.0, -1.0).astype(jnp.float32)
    loss = jax.nn.softplus(-label * logit)
    slope = -label * jax.nn.sigmoid(-label * logit)
    dcos = LOGIT_SCALE / width * slope[:, None]
    dunit = dcos * normed
    dnormed = dcos * unit
    dpool = pnorm * (dunit - unit * jnp.mean(dunit * unit, -1, keepdims=True))
    dout = dpool.astype(jnp.bfloat16).reshape(count, HEADS, depth)
    dattn = jnp.einsum("chd,phd->chp", dout, patch_values, preferred_element_type=jnp.float32)
    grad_v = jnp.einsum("chp,chd->phd", attn, dout, preferred_element_type=jnp.float32).reshape(
        -1, width
    )
    dscore = (
        weights * (dattn - jnp.sum(weights * dattn, -1, keepdims=True)) * depth ** (-0.5)
    ).astype(jnp.bfloat16)
    grad_q = jnp.einsum(
        "chp,phd->chd", dscore, patch_keys, preferred_element_type=jnp.float32
    ).reshape(count, width)
    grad_k = jnp.einsum(
        "chp,chd->phd", dscore, queries, preferred_element_type=jnp.float32
    ).reshape(-1, width)
    grad_x = grad_q + tnorm * (dnormed - normed * jnp.mean(dnormed * normed, -1, keepdims=True))
    return (loss, grad_x, grad_k, grad_v)


def pair_block(block_text, pair_image, first_caption, keys, values, first_image):
    count = block_text.shape[0]
    width = block_text.shape[1]
    text_wide = block_text.astype(jnp.float32)
    tnorm = lax.rsqrt(jnp.mean(text_wide * text_wide, -1, keepdims=True) + EPS)
    normed = text_wide * tnorm
    pairs = lax.dynamic_slice_in_dim(pair_image, first_caption, count)
    image_ids = first_image + jnp.arange(keys.shape[0], dtype=jnp.int32)

    def one_image(carry, item):
        keys_one, values_one, image_id = item
        loss, grad_x, grad_k, grad_v = image_terms(
            block_text, normed, tnorm, pairs, image_id, keys_one, values_one
        )
        return ((carry[0] + loss, carry[1] + grad_x), (grad_k, grad_v))

    start = (jnp.zeros((count,), jnp.float32), jnp.zeros((count, width), jnp.float32))
    (loss_sum, grad_text), (grad_keys, grad_values) = lax.scan(
        one_image, start, (keys, values, image_ids)
    )
    return (loss_sum, grad_text, grad_keys, grad_values)


def local(text, keys, values, pair_image):
    image = lax.axis_index(PLANE + LINE)
    image_total = lax.axis_size(PLANE + LINE)
    all_text = gathered(gathered(text, LINE), PLANE)
    loss, grad, grad_keys, grad_values = pair_block(
        all_text, pair_image, 0, keys, values, image * keys.shape[0]
    )
    width = text.shape[1]
    sums = jnp.concatenate([grad, jnp.broadcast_to(loss[:, None], (loss.shape[0], 128))], axis=1)
    sums = scattered_sum(sums.astype(jnp.bfloat16), PLANE)
    sums = scattered_sum(sums, LINE)
    return (sums[:, width] / image_total, sums[:, :width], grad_keys, grad_values)


def solution(mesh):
    torus = Mesh(mesh.devices.reshape(4, 8, 16), ("blk", "row", "line"))
    over = PLANE + LINE
    in_specs = (P(over, None), P(over, None, None), P(over, None, None), P())
    out_specs = (P(over), P(over, None), P(over, None, None), P(over, None, None))
    return jax.shard_map(local, mesh=torus, in_specs=in_specs, out_specs=out_specs, check_vma=False)
```

```python
import functools

import jax
import jax.numpy as jnp
from jax import lax
from jax.experimental import pallas as pl
from jax.experimental.pallas import tpu as pltpu
from jax.sharding import Mesh
from jax.sharding import PartitionSpec as P

HEADS = 8
OVER = ("x_lo", "core", "x_hi", "y", "z")
PLANE = ("x_lo", "x_hi", "y")
LINE = ("core", "z")


EPS = 1e-06
LOGIT_SCALE = 10.0
LOGIT_BIAS = -1.0
LANES = 128
LOSS_LANES = 128
VMEM_BYTES = 24 << 20
SMALL_BYTES = 4 << 20


def exchanged(parts, axes):
    return lax.all_to_all(parts, axes, 0, 0, tiled=True)


def copies_kernel(row_ref, copies_ref):
    count, blocks, lanes = copies_ref.shape
    row = row_ref[...].astype(jnp.float32)
    cut = [row[:, lanes * block : lanes * (block + 1)] for block in range(blocks)]
    cut = jnp.concatenate(cut, axis=0).astype(jnp.bfloat16)
    copies_ref[...] = jnp.broadcast_to(cut[None], copies_ref.shape)


def rows_kernel(cut_ref, copies_ref):
    cut = cut_ref[...].astype(jnp.float32)
    rows = [cut[:, block] for block in range(cut.shape[1])]
    rows = jnp.concatenate(rows, axis=1).astype(jnp.bfloat16)
    copies_ref[...] = jnp.broadcast_to(rows[None], copies_ref.shape)


def total_kernel(image_total, parts_ref, loss_ref, grad_ref):
    width = grad_ref.shape[1]
    total = jnp.sum(parts_ref[...], axis=0)
    grad_ref[...] = total[:, :width]
    loss_ref[...] = total[:, width : width + 1] * (1.0 / image_total)


def gathered(row):
    width = row.shape[1]
    line, plane = lax.axis_size(LINE), lax.axis_size(PLANE)
    inside = pl.BlockSpec(memory_space=pltpu.VMEM)
    copies = pl.pallas_call(
        copies_kernel,
        out_shape=jax.ShapeDtypeStruct((line, width // LANES, LANES), row.dtype),
        in_specs=[inside],
        out_specs=inside,
        compiler_params=pltpu.CompilerParams(vmem_limit_bytes=SMALL_BYTES),
        name="copies",
    )(row)
    rows = pl.pallas_call(
        rows_kernel,
        out_shape=jax.ShapeDtypeStruct((plane, line, width), row.dtype),
        in_specs=[inside],
        out_specs=inside,
        compiler_params=pltpu.CompilerParams(vmem_limit_bytes=SMALL_BYTES),
        name="rows",
    )(exchanged(copies, LINE))
    return exchanged(rows, PLANE).reshape(-1, width)


def summed(rows, image_total, width):
    plane = PLANE + LINE[:1]
    parts = rows.reshape(lax.axis_size(plane), -1, rows.shape[1])
    parts = jnp.sum(exchanged(parts, plane).astype(jnp.float32), axis=0)
    parts = exchanged(parts[:, None], LINE[1:])
    inside = pl.BlockSpec(memory_space=pltpu.VMEM)
    return pl.pallas_call(
        functools.partial(total_kernel, image_total),
        out_shape=(
            jax.ShapeDtypeStruct((1, 1), jnp.float32),
            jax.ShapeDtypeStruct((1, width), jnp.float32),
        ),
        in_specs=[inside],
        out_specs=(inside, inside),
        compiler_params=pltpu.CompilerParams(vmem_limit_bytes=SMALL_BYTES),
        name="total",
    )(parts)


def gathered_place(caption, sizes):
    index = {}
    for axis, size in reversed(tuple(zip(OVER, sizes))):
        index[axis] = lax.rem(caption, size)
        caption = lax.div(caption, size)
    place = jnp.zeros_like(caption)
    for axis in PLANE + LINE:
        place = place * sizes[OVER.index(axis)] + index[axis]
    return place


def padded_head(rows, head):
    zeros = jnp.zeros_like(rows)
    return jnp.concatenate([rows, zeros] if head % 2 == 0 else [zeros, rows], axis=0)


def pair_of(head, depth):
    first = head // 2 * 2 * depth
    return slice(first, first + 2 * depth)


def pair_kernel(
    sizes, image_ref, pairs_ref, text_ref, keys_ref, values_ref,
    sums_ref, keys_out, values_out,
    keys_t_in, values_t_in,
    text_t, dout_t, attn, dscore, weights, pooled, grad_keys, grad_values, left,
):
    count, width = text_ref.shape
    patches = keys_ref.shape[0]
    depth = width // HEADS
    scale = depth ** (-0.5)
    text_t[...] = text_ref[...].T
    wide = text_t[...].astype(jnp.float32)
    tnorm = lax.rsqrt(jnp.mean(wide * wide, 0, keepdims=True) + EPS)
    values_t_in[...] = values_ref[...].T
    for head in range(HEADS):
        rows = slice(head * depth, (head + 1) * depth)
        query = text_t[rows, :] * jnp.asarray(scale, jnp.bfloat16)
        scores = jnp.dot(
            keys_ref[:, pair_of(head, depth)],
            padded_head(query, head),
            preferred_element_type=jnp.float32,
        )
        grown = jnp.exp(scores - jnp.max(scores, 0, keepdims=True))
        weight = grown * (1.0 / jnp.sum(grown, 0, keepdims=True))
        weights[head] = weight
        attn[head] = weight.astype(jnp.bfloat16)
        pooled[rows, :] = jnp.dot(
            values_t_in[rows, :], attn[head], preferred_element_type=jnp.float32
        )
    keys_t_in[...] = keys_ref[...].T
    pool = pooled[...]
    pnorm = lax.rsqrt(jnp.mean(pool * pool, 0, keepdims=True) + EPS)
    cosine = jnp.mean(pool * wide, 0, keepdims=True) * pnorm * tnorm
    logit = LOGIT_SCALE * cosine + LOGIT_BIAS
    captions = lax.broadcasted_iota(jnp.int32, (1, count), 1)
    described = jnp.where(pairs_ref[...] == image_ref[0], captions, 0)
    matching = gathered_place(jnp.sum(described, 1, keepdims=True), sizes)
    label = jnp.where(captions == matching, 1.0, -1.0).astype(jnp.float32)
    margin = -label * logit
    loss = jnp.maximum(margin, 0.0) + jnp.log1p(jnp.exp(-jnp.abs(margin)))
    slope = -label / (1.0 + jnp.exp(-margin))
    dcos = LOGIT_SCALE / width * slope
    dout_t[...] = (
        (pnorm * dcos * tnorm) * wide - (pnorm * dcos * cosine * pnorm) * pool
    ).astype(jnp.bfloat16)
    pooled[...] = (tnorm * dcos * pnorm) * pool - (tnorm * dcos * cosine * tnorm) * wide

    def over_captions(parts, rows_t, head):
        return lax.dot_general(
            parts[head],
            padded_head(rows_t[head * depth : (head + 1) * depth, :], head),
            (((1,), (1,)), ((), ())),
            preferred_element_type=jnp.float32,
        )

    blocks = HEADS // 2
    for block in range(blocks):
        lines = pl.ds(block, patches, stride=blocks)
        for head in (2 * block, 2 * block + 1):
            rows = slice(head * depth, (head + 1) * depth)
            dattn = jnp.dot(
                values_ref[:, pair_of(head, depth)],
                padded_head(dout_t[rows, :], head),
                preferred_element_type=jnp.float32,
            )
            weight = weights[head]
            carried = jnp.sum(weight * dattn, 0, keepdims=True)
            dscore[head] = (weight * scale * (dattn - carried)).astype(jnp.bfloat16)
            pooled[rows, :] += jnp.dot(
                keys_t_in[rows, :], dscore[head], preferred_element_type=jnp.float32
            )
        grad_values[lines, :] = over_captions(attn, dout_t, 2 * block) + over_captions(
            attn, dout_t, 2 * block + 1
        )
        grad_keys[lines, :] = over_captions(dscore, text_t, 2 * block) + over_captions(
            dscore, text_t, 2 * block + 1
        )
    values_copy = pltpu.make_async_copy(grad_values, values_out, left.at[0])
    keys_copy = pltpu.make_async_copy(grad_keys, keys_out, left.at[1])
    values_copy.start()
    keys_copy.start()
    sums_ref[:, :width] = pooled[...].T.astype(jnp.bfloat16)
    sums_ref[:, width:] = jnp.broadcast_to(loss, (LOSS_LANES, count)).T.astype(jnp.bfloat16)
    values_copy.wait()
    keys_copy.wait()


def one_image(sizes, image, pairs, all_text, keys, values):
    patches, width = keys.shape[1:]
    count = all_text.shape[0]
    flops = 2 * count * patches * width
    lines = (patches * HEADS // 2, 2 * width // HEADS)
    inside = pl.BlockSpec(memory_space=pltpu.VMEM)
    anywhere = pl.BlockSpec(memory_space=pl.ANY)
    tall_text = pltpu.VMEM((width, count), jnp.bfloat16)
    tall_image = pltpu.VMEM((width, patches), jnp.bfloat16)
    per_head = pltpu.VMEM((HEADS, patches, count), jnp.bfloat16)
    sums, grad_keys, grad_values = pl.pallas_call(
        functools.partial(pair_kernel, sizes),
        out_shape=(
            jax.ShapeDtypeStruct((count, width + LOSS_LANES), jnp.bfloat16),
            jax.ShapeDtypeStruct(lines, jnp.float32),
            jax.ShapeDtypeStruct(lines, jnp.float32),
        ),
        in_specs=[
            pl.BlockSpec(memory_space=pltpu.SMEM),
            *[inside] * 4,
        ],
        out_specs=(inside, anywhere, anywhere),
        scratch_shapes=[
            tall_image,
            tall_image,
            tall_text,
            tall_text,
            per_head,
            per_head,
            pltpu.VMEM((HEADS, patches, count), jnp.float32),
            pltpu.VMEM((width, count), jnp.float32),
            pltpu.VMEM(lines, jnp.float32),
            pltpu.VMEM(lines, jnp.float32),
            pltpu.SemaphoreType.DMA((2,)),
        ],
        compiler_params=pltpu.CompilerParams(vmem_limit_bytes=VMEM_BYTES),
        cost_estimate=pl.CostEstimate(
            flops=6 * flops, bytes_accessed=3 << 20, transcendentals=HEADS * patches * count
        ),
        name="pairs",
    )(image, pairs, all_text, keys[0], values[0])
    return sums, grad_keys.reshape(keys.shape), grad_values.reshape(values.shape)


def local(text, keys, values, pair_image):
    width = text.shape[1]
    image = lax.axis_index(OVER)
    image_total = lax.axis_size(OVER)
    all_text = gathered(text)
    sums, grad_keys, grad_values = one_image(
        tuple(lax.axis_size(axis) for axis in OVER),
        image.astype(jnp.int32).reshape(1),
        pair_image.reshape(1, -1),
        all_text,
        keys,
        values,
    )
    loss, grad_text = summed(sums, image_total, width)
    return (loss.reshape(1), grad_text, grad_keys, grad_values)


def solution(mesh):
    torus = Mesh(mesh.devices.reshape(2, 2, 2, 4, 16), OVER)
    in_specs = (P(OVER, None), P(OVER, None, None), P(OVER, None, None), P())
    out_specs = (P(OVER), P(OVER, None), P(OVER, None, None), P(OVER, None, None))
    return jax.shard_map(local, mesh=torus, in_specs=in_specs, out_specs=out_specs, check_vma=False)
```

```python
import functools

import jax
import jax.numpy as jnp
from jax import lax
from jax.experimental import pallas as pl
from jax.experimental.pallas import tpu as pltpu
from jax.sharding import Mesh
from jax.sharding import PartitionSpec as P

HEADS = 8
OVER = ("x_lo", "core", "x_hi", "y", "z")
PLANE = ("x_lo", "x_hi", "y")
LINE = ("core", "z")


EPS = 1e-06
LOGIT_SCALE = 10.0
LOGIT_BIAS = -1.0
LANES = 128
LOSS_LANES = 128
VMEM_BYTES = 24 << 20
SMALL_BYTES = 4 << 20


def exchanged(parts, axes):
    return lax.all_to_all(parts, axes, 0, 0, tiled=True)


def copies_kernel(row_ref, copies_ref):
    count, blocks, lanes = copies_ref.shape
    row = row_ref[...].astype(jnp.float32)
    cut = [row[:, lanes * block : lanes * (block + 1)] for block in range(blocks)]
    cut = jnp.concatenate(cut, axis=0).astype(jnp.bfloat16)
    copies_ref[...] = jnp.broadcast_to(cut[None], copies_ref.shape)


def rows_kernel(cut_ref, copies_ref):
    cut = cut_ref[...].astype(jnp.float32)
    rows = [cut[:, block] for block in range(cut.shape[1])]
    rows = jnp.concatenate(rows, axis=1).astype(jnp.bfloat16)
    copies_ref[...] = jnp.broadcast_to(rows[None], copies_ref.shape)


def total_kernel(image_total, parts_ref, loss_ref, grad_ref):
    width = grad_ref.shape[1]
    total = jnp.sum(parts_ref[...], axis=0)
    grad_ref[...] = total[:, :width]
    loss_ref[...] = total[:, width : width + 1] * (1.0 / image_total)


def gathered(row):
    width = row.shape[1]
    line, plane = lax.axis_size(LINE), lax.axis_size(PLANE)
    inside = pl.BlockSpec(memory_space=pltpu.VMEM)
    copies = pl.pallas_call(
        copies_kernel,
        out_shape=jax.ShapeDtypeStruct((line, width // LANES, LANES), row.dtype),
        in_specs=[inside],
        out_specs=inside,
        compiler_params=pltpu.CompilerParams(vmem_limit_bytes=SMALL_BYTES),
        name="copies",
    )(row)
    rows = pl.pallas_call(
        rows_kernel,
        out_shape=jax.ShapeDtypeStruct((plane, line, width), row.dtype),
        in_specs=[inside],
        out_specs=inside,
        compiler_params=pltpu.CompilerParams(vmem_limit_bytes=SMALL_BYTES),
        name="rows",
    )(exchanged(copies, LINE))
    return exchanged(rows, PLANE).reshape(-1, width)


def summed(own, other, second, image_total, width):
    both = lax.all_gather(other, LINE[0], axis=0)
    swapped = jnp.where(second > 0, both[0], both[1])
    parts = (own.astype(jnp.float32) + swapped.astype(jnp.float32)).astype(own.dtype)
    parts = jnp.sum(exchanged(parts, PLANE).astype(jnp.float32), axis=0)
    parts = exchanged(parts[:, None], LINE[1:])
    inside = pl.BlockSpec(memory_space=pltpu.VMEM)
    return pl.pallas_call(
        functools.partial(total_kernel, image_total),
        out_shape=(
            jax.ShapeDtypeStruct((1, 1), jnp.float32),
            jax.ShapeDtypeStruct((1, width), jnp.float32),
        ),
        in_specs=[inside],
        out_specs=(inside, inside),
        compiler_params=pltpu.CompilerParams(vmem_limit_bytes=SMALL_BYTES),
        name="total",
    )(parts)


def gathered_place(caption, sizes):
    index = {}
    for axis, size in reversed(tuple(zip(OVER, sizes))):
        index[axis] = lax.rem(caption, size)
        caption = lax.div(caption, size)
    place = jnp.zeros_like(caption)
    for axis in PLANE + LINE:
        place = place * sizes[OVER.index(axis)] + index[axis]
    return place


def padded_head(rows, head):
    zeros = jnp.zeros_like(rows)
    return jnp.concatenate([rows, zeros] if head % 2 == 0 else [zeros, rows], axis=0)


def pair_kernel(
    sizes, pairs_ref, text_ref, keys_ref, values_ref,
    own_ref, other_ref, second_ref, keys_out, values_out,
    keys_t, values_t, text_t, dout_t, attn, dscore, weights, pooled, sums,
    grad_keys, grad_values, pairs_in, arrived, left,
):
    pairs_copy = pltpu.make_async_copy(pairs_ref, pairs_in, arrived)
    pairs_copy.start()
    count, width = text_ref.shape
    patches = keys_ref.shape[0]
    depth = width // HEADS
    scale = depth ** (-0.5)
    blocks = HEADS // 2
    text_square = pool_square = pool_text = jnp.zeros((1, count), jnp.float32)
    for block in range(blocks):
        lanes = slice(2 * block * depth, 2 * (block + 1) * depth)
        text_t[lanes, :] = text_ref[:, lanes].T
        values_t[lanes, :] = values_ref[:, lanes].T
        for head in (2 * block, 2 * block + 1):
            rows = slice(head * depth, (head + 1) * depth)
            query = text_t[rows, :]
            scores = jnp.dot(
                keys_ref[:, lanes],
                padded_head(query * jnp.asarray(scale, query.dtype), head),
                preferred_element_type=jnp.float32,
            )
            grown = jnp.exp(scores - jnp.max(scores, 0, keepdims=True))
            weight = grown * (1.0 / jnp.sum(grown, 0, keepdims=True))
            weights[head] = weight
            attn[head] = weight.astype(jnp.bfloat16)
            pool = jnp.dot(values_t[rows, :], attn[head], preferred_element_type=jnp.float32)
            pooled[rows, :] = pool
            wide = query.astype(jnp.float32)
            text_square += jnp.sum(wide * wide, 0, keepdims=True)
            pool_square += jnp.sum(pool * pool, 0, keepdims=True)
            pool_text += jnp.sum(pool * wide, 0, keepdims=True)
    tnorm = lax.rsqrt(text_square * (1.0 / width) + EPS)
    pnorm = lax.rsqrt(pool_square * (1.0 / width) + EPS)
    cosine = pool_text * (1.0 / width) * pnorm * tnorm
    logit = LOGIT_SCALE * cosine + LOGIT_BIAS
    captions = lax.broadcasted_iota(jnp.int32, (1, count), 1)
    pairs_copy.wait()
    described = jnp.where(pairs_in[...] == lax.axis_index(OVER), captions, 0)
    matching = gathered_place(jnp.sum(described, 1, keepdims=True), sizes)
    label = jnp.where(captions == matching, 1.0, -1.0).astype(jnp.float32)
    margin = -label * logit
    loss = jnp.maximum(margin, 0.0) + jnp.log1p(jnp.exp(-jnp.abs(margin)))
    slope = -label / (1.0 + jnp.exp(-margin))
    dcos = LOGIT_SCALE / width * slope
    out_text, out_pool = pnorm * dcos * tnorm, pnorm * dcos * cosine * pnorm
    direct_pool, direct_text = tnorm * dcos * pnorm, tnorm * dcos * cosine * tnorm

    def over_captions(parts, rows_t, head):
        return lax.dot_general(
            parts[head],
            padded_head(rows_t[head * depth : (head + 1) * depth, :], head),
            (((1,), (1,)), ((), ())),
            preferred_element_type=jnp.float32,
        )

    parts = (sizes[0] * sizes[2] * sizes[3], sizes[1], sizes[4])
    for block in range(blocks):
        lanes = slice(2 * block * depth, 2 * (block + 1) * depth)
        keys_t[lanes, :] = keys_ref[:, lanes].T
        for head in (2 * block, 2 * block + 1):
            rows = slice(head * depth, (head + 1) * depth)
            wide = text_t[rows, :].astype(jnp.float32)
            pool = pooled[rows, :]
            dout = (out_text * wide - out_pool * pool).astype(jnp.bfloat16)
            dout_t[rows, :] = dout
            dattn = jnp.dot(
                values_ref[:, lanes], padded_head(dout, head), preferred_element_type=jnp.float32
            )
            weight = weights[head]
            carried = jnp.sum(weight * dattn, 0, keepdims=True)
            dscore[head] = (weight * scale * (dattn - carried)).astype(jnp.bfloat16)
            pooled[rows, :] = (direct_pool * pool - direct_text * wide) + jnp.dot(
                keys_t[rows, :], dscore[head], preferred_element_type=jnp.float32
            )
        sums[..., lanes] = pooled[lanes, :].T.astype(jnp.bfloat16).reshape(*parts, 2 * depth)
        lines = pl.ds(block, patches, stride=blocks)
        grad_values[lines, :] = over_captions(attn, dout_t, 2 * block) + over_captions(
            attn, dout_t, 2 * block + 1
        )
        grad_keys[lines, :] = over_captions(dscore, text_t, 2 * block) + over_captions(
            dscore, text_t, 2 * block + 1
        )
    values_copy = pltpu.make_async_copy(grad_values, values_out, left.at[0])
    keys_copy = pltpu.make_async_copy(grad_keys, keys_out, left.at[1])
    values_copy.start()
    keys_copy.start()
    losses = jnp.broadcast_to(loss, (LOSS_LANES, count)).T.astype(jnp.bfloat16)
    sums[..., width:] = losses.reshape(*parts, LOSS_LANES)
    core = lax.axis_index(LINE[0])
    own_ref[...] = sums[:, core]
    other_ref[...] = sums[:, 1 - core]
    second_ref[...] = jnp.full(second_ref.shape, core, jnp.float32)
    values_copy.wait()
    keys_copy.wait()


def one_image(sizes, pairs, all_text, keys, values):
    patches, width = keys.shape[1:]
    count = all_text.shape[0]
    flops = 2 * count * patches * width
    lines = (patches * HEADS // 2, 2 * width // HEADS)
    apart = (sizes[0] * sizes[2] * sizes[3], sizes[4], width + LOSS_LANES)
    inside = pl.BlockSpec(memory_space=pltpu.VMEM)
    anywhere = pl.BlockSpec(memory_space=pl.ANY)
    tall_text = pltpu.VMEM((width, count), jnp.bfloat16)
    tall_image = pltpu.VMEM((width, patches), jnp.bfloat16)
    per_head = pltpu.VMEM((HEADS, patches, count), jnp.bfloat16)
    own, other, second, grad_keys, grad_values = pl.pallas_call(
        functools.partial(pair_kernel, sizes),
        out_shape=(
            jax.ShapeDtypeStruct(apart, jnp.bfloat16),
            jax.ShapeDtypeStruct(apart, jnp.bfloat16),
            jax.ShapeDtypeStruct((1, apart[2]), jnp.float32),
            jax.ShapeDtypeStruct(lines, jnp.float32),
            jax.ShapeDtypeStruct(lines, jnp.float32),
        ),
        in_specs=[
            anywhere,
            *[inside] * 3,
        ],
        out_specs=(inside, inside, inside, anywhere, anywhere),
        scratch_shapes=[
            tall_image,
            tall_image,
            tall_text,
            tall_text,
            per_head,
            per_head,
            pltpu.VMEM((HEADS, patches, count), jnp.float32),
            pltpu.VMEM((width, count), jnp.float32),
            pltpu.VMEM((apart[0], sizes[1], *apart[1:]), jnp.bfloat16),
            pltpu.VMEM(lines, jnp.float32),
            pltpu.VMEM(lines, jnp.float32),
            pltpu.VMEM(pairs.shape, pairs.dtype),
            pltpu.SemaphoreType.DMA(()),
            pltpu.SemaphoreType.DMA((2,)),
        ],
        compiler_params=pltpu.CompilerParams(vmem_limit_bytes=VMEM_BYTES),
        cost_estimate=pl.CostEstimate(
            flops=6 * flops, bytes_accessed=3 << 20, transcendentals=HEADS * patches * count
        ),
        name="pairs",
    )(pltpu.with_memory_space_constraint(pairs, pltpu.HBM), all_text, keys[0], values[0])
    return own, other, second, grad_keys.reshape(keys.shape), grad_values.reshape(values.shape)


def local(text, keys, values, pair_image):
    width = text.shape[1]
    image_total = lax.axis_size(OVER)
    all_text = gathered(text)
    own, other, second, grad_keys, grad_values = one_image(
        tuple(lax.axis_size(axis) for axis in OVER),
        pair_image.reshape(1, -1),
        all_text,
        keys,
        values,
    )
    loss, grad_text = summed(own, other, second, image_total, width)
    return (loss.reshape(1), grad_text, grad_keys, grad_values)


def solution(mesh):
    torus = Mesh(mesh.devices.reshape(2, 2, 2, 4, 16), OVER)
    in_specs = (P(OVER, None), P(OVER, None, None), P(OVER, None, None), P())
    out_specs = (P(OVER), P(OVER, None), P(OVER, None, None), P(OVER, None, None))
    return jax.shard_map(local, mesh=torus, in_specs=in_specs, out_specs=out_specs, check_vma=False)
```

```python
import functools

import jax
import jax.numpy as jnp
from jax import lax
from jax.experimental import pallas as pl
from jax.experimental.pallas import tpu as pltpu
from jax.sharding import Mesh
from jax.sharding import PartitionSpec as P

HEADS = 8
OVER = ("x_lo", "core", "x_hi", "y", "z")
PLANE = ("x_lo", "x_hi", "y")
LINE = ("core", "z")


EPS = 1e-06
LOGIT_SCALE = 10.0
LOGIT_BIAS = -1.0
LANES = 128
LOSS_LANES = 128
VMEM_BYTES = 24 << 20
SMALL_BYTES = 4 << 20


def exchanged(parts, axes):
    return lax.all_to_all(parts, axes, 0, 0, tiled=True)


def copies_kernel(row_ref, copies_ref):
    count, blocks, lanes = copies_ref.shape
    row = row_ref[...].astype(jnp.float32)
    cut = [row[:, lanes * block : lanes * (block + 1)] for block in range(blocks)]
    cut = jnp.concatenate(cut, axis=0).astype(jnp.bfloat16)
    copies_ref[...] = jnp.broadcast_to(cut[None], copies_ref.shape)


def rows_kernel(cut_ref, copies_ref):
    cut = cut_ref[...].astype(jnp.float32)
    rows = [cut[:, block] for block in range(cut.shape[1])]
    rows = jnp.concatenate(rows, axis=1).astype(jnp.bfloat16)
    copies_ref[...] = jnp.broadcast_to(rows[None], copies_ref.shape)


def total_kernel(image_total, parts_ref, loss_ref, grad_ref):
    width = grad_ref.shape[1]
    total = jnp.sum(parts_ref[...], axis=0)
    grad_ref[...] = total[:, :width]
    loss_ref[...] = total[:, width : width + 1] * (1.0 / image_total)


def gathered(row):
    width = row.shape[1]
    line, plane = lax.axis_size(LINE), lax.axis_size(PLANE)
    inside = pl.BlockSpec(memory_space=pltpu.VMEM)
    copies = pl.pallas_call(
        copies_kernel,
        out_shape=jax.ShapeDtypeStruct((line, width // LANES, LANES), row.dtype),
        in_specs=[inside],
        out_specs=inside,
        compiler_params=pltpu.CompilerParams(vmem_limit_bytes=SMALL_BYTES),
        name="copies",
    )(row)
    rows = pl.pallas_call(
        rows_kernel,
        out_shape=jax.ShapeDtypeStruct((plane, line, width), row.dtype),
        in_specs=[inside],
        out_specs=inside,
        compiler_params=pltpu.CompilerParams(vmem_limit_bytes=SMALL_BYTES),
        name="rows",
    )(exchanged(copies, LINE))
    return exchanged(rows, PLANE).reshape(-1, width)


def summed(own, other, second, image_total, width):
    both = lax.all_gather(other, LINE[0], axis=0)
    swapped = jnp.where(second > 0, both[0], both[1])
    parts = (own.astype(jnp.float32) + swapped.astype(jnp.float32)).astype(own.dtype)
    parts = jnp.sum(exchanged(parts, PLANE).astype(jnp.float32), axis=0)
    parts = exchanged(parts[:, None], LINE[1:])
    inside = pl.BlockSpec(memory_space=pltpu.VMEM)
    return pl.pallas_call(
        functools.partial(total_kernel, image_total),
        out_shape=(
            jax.ShapeDtypeStruct((1, 1), jnp.float32),
            jax.ShapeDtypeStruct((1, width), jnp.float32),
        ),
        in_specs=[inside],
        out_specs=(inside, inside),
        compiler_params=pltpu.CompilerParams(vmem_limit_bytes=SMALL_BYTES),
        name="total",
    )(parts)


def gathered_place(caption, sizes):
    index = {}
    for axis, size in reversed(tuple(zip(OVER, sizes))):
        index[axis] = lax.rem(caption, size)
        caption = lax.div(caption, size)
    place = jnp.zeros_like(caption)
    for axis in PLANE + LINE:
        place = place * sizes[OVER.index(axis)] + index[axis]
    return place


def padded_head(rows, head):
    zeros = jnp.zeros_like(rows)
    return jnp.concatenate([rows, zeros] if head % 2 == 0 else [zeros, rows], axis=0)


def pair_kernel(
    sizes, pairs_ref, text_ref, keys_ref, values_ref,
    own_ref, other_ref, second_ref, keys_out, values_out,
    keys_t, values_t, text_t, dout_t, attn, dscore, weights, pooled, sums,
    grad_keys, grad_values, pairs_in, arrived, left,
):
    pairs_copy = pltpu.make_async_copy(pairs_ref, pairs_in, arrived)
    pairs_copy.start()
    count, width = text_ref.shape
    patches = keys_ref.shape[0]
    depth = width // HEADS
    scale = depth ** (-0.5)
    blocks = HEADS // 2
    text_square = pool_square = pool_text = jnp.zeros((1, count), jnp.float32)
    def rows_of(head):
        return slice(head * depth, (head + 1) * depth)

    def lanes_of(head):
        return slice(head // 2 * 2 * depth, (head // 2 + 1) * 2 * depth)

    def scored(head):
        lanes = lanes_of(head)
        if head % 2 == 0:
            text_t[lanes, :] = text_ref[:, lanes].T
            values_t[lanes, :] = values_ref[:, lanes].T
        query = text_t[rows_of(head), :]
        return jnp.dot(
            keys_ref[:, lanes],
            padded_head(query * jnp.asarray(scale, query.dtype), head),
            preferred_element_type=jnp.float32,
        )

    scores = [scored(head) for head in range(HEADS)]
    for head in range(HEADS + 1):
        if head > 0:
            rows = rows_of(head - 1)
            pool = jnp.dot(values_t[rows, :], attn[head - 1], preferred_element_type=jnp.float32)
            pooled[rows, :] = pool
            wide = text_t[rows, :].astype(jnp.float32)
            text_square += jnp.sum(wide * wide, 0, keepdims=True)
            pool_square += jnp.sum(pool * pool, 0, keepdims=True)
            pool_text += jnp.sum(pool * wide, 0, keepdims=True)
        if head < HEADS:
            grown = jnp.exp(scores[head] - jnp.max(scores[head], 0, keepdims=True))
            weight = grown * (1.0 / jnp.sum(grown, 0, keepdims=True))
            weights[head] = weight
            attn[head] = weight.astype(jnp.bfloat16)
    tnorm = lax.rsqrt(text_square * (1.0 / width) + EPS)
    pnorm = lax.rsqrt(pool_square * (1.0 / width) + EPS)
    cosine = pool_text * (1.0 / width) * pnorm * tnorm
    logit = LOGIT_SCALE * cosine + LOGIT_BIAS
    captions = lax.broadcasted_iota(jnp.int32, (1, count), 1)
    pairs_copy.wait()
    described = jnp.where(pairs_in[...] == lax.axis_index(OVER), captions, 0)
    matching = gathered_place(jnp.sum(described, 1, keepdims=True), sizes)
    label = jnp.where(captions == matching, 1.0, -1.0).astype(jnp.float32)
    margin = -label * logit
    loss = jnp.maximum(margin, 0.0) + jnp.log1p(jnp.exp(-jnp.abs(margin)))
    slope = -label / (1.0 + jnp.exp(-margin))
    dcos = LOGIT_SCALE / width * slope
    out_text, out_pool = pnorm * dcos * tnorm, pnorm * dcos * cosine * pnorm
    direct_pool, direct_text = tnorm * dcos * pnorm, tnorm * dcos * cosine * tnorm

    def over_captions(parts, rows_t, head):
        return lax.dot_general(
            parts[head],
            padded_head(rows_t[head * depth : (head + 1) * depth, :], head),
            (((1,), (1,)), ((), ())),
            preferred_element_type=jnp.float32,
        )

    parts = (sizes[0] * sizes[2] * sizes[3], sizes[1], sizes[4])
    def attended(head):
        lanes, rows = lanes_of(head), rows_of(head)
        if head % 2 == 0:
            keys_t[lanes, :] = keys_ref[:, lanes].T
        wide = text_t[rows, :].astype(jnp.float32)
        pool = pooled[rows, :]
        dout = (out_text * wide - out_pool * pool).astype(jnp.bfloat16)
        dout_t[rows, :] = dout
        pooled[rows, :] = direct_pool * pool - direct_text * wide
        return jnp.dot(
            values_ref[:, lanes], padded_head(dout, head), preferred_element_type=jnp.float32
        )

    dattn = [attended(head) for head in range(HEADS)]
    for head in range(HEADS + 1):
        if head > 0:
            rows = rows_of(head - 1)
            pooled[rows, :] += jnp.dot(
                keys_t[rows, :], dscore[head - 1], preferred_element_type=jnp.float32
            )
        if head > 0 and head % 2 == 0:
            block = head // 2 - 1
            lanes = lanes_of(head - 1)
            sums[..., lanes] = pooled[lanes, :].T.astype(jnp.bfloat16).reshape(*parts, 2 * depth)
            lines = pl.ds(block, patches, stride=blocks)
            grad_values[lines, :] = over_captions(attn, dout_t, 2 * block) + over_captions(
                attn, dout_t, 2 * block + 1
            )
            grad_keys[lines, :] = over_captions(dscore, text_t, 2 * block) + over_captions(
                dscore, text_t, 2 * block + 1
            )
        if head < HEADS:
            weight = weights[head]
            carried = jnp.sum(weight * dattn[head], 0, keepdims=True)
            dscore[head] = (weight * scale * (dattn[head] - carried)).astype(jnp.bfloat16)
    values_copy = pltpu.make_async_copy(grad_values, values_out, left.at[0])
    keys_copy = pltpu.make_async_copy(grad_keys, keys_out, left.at[1])
    values_copy.start()
    keys_copy.start()
    losses = jnp.broadcast_to(loss, (LOSS_LANES, count)).T.astype(jnp.bfloat16)
    sums[..., width:] = losses.reshape(*parts, LOSS_LANES)
    core = lax.axis_index(LINE[0])
    own_ref[...] = sums[:, core]
    other_ref[...] = sums[:, 1 - core]
    second_ref[...] = jnp.full(second_ref.shape, core, jnp.float32)
    values_copy.wait()
    keys_copy.wait()


def one_image(sizes, pairs, all_text, keys, values):
    patches, width = keys.shape[1:]
    count = all_text.shape[0]
    flops = 2 * count * patches * width
    lines = (patches * HEADS // 2, 2 * width // HEADS)
    apart = (sizes[0] * sizes[2] * sizes[3], sizes[4], width + LOSS_LANES)
    inside = pl.BlockSpec(memory_space=pltpu.VMEM)
    anywhere = pl.BlockSpec(memory_space=pl.ANY)
    tall_text = pltpu.VMEM((width, count), jnp.bfloat16)
    tall_image = pltpu.VMEM((width, patches), jnp.bfloat16)
    per_head = pltpu.VMEM((HEADS, patches, count), jnp.bfloat16)
    own, other, second, grad_keys, grad_values = pl.pallas_call(
        functools.partial(pair_kernel, sizes),
        out_shape=(
            jax.ShapeDtypeStruct(apart, jnp.bfloat16),
            jax.ShapeDtypeStruct(apart, jnp.bfloat16),
            jax.ShapeDtypeStruct((1, apart[2]), jnp.float32),
            jax.ShapeDtypeStruct(lines, jnp.float32),
            jax.ShapeDtypeStruct(lines, jnp.float32),
        ),
        in_specs=[
            anywhere,
            *[inside] * 3,
        ],
        out_specs=(inside, inside, inside, anywhere, anywhere),
        scratch_shapes=[
            tall_image,
            tall_image,
            tall_text,
            tall_text,
            per_head,
            per_head,
            pltpu.VMEM((HEADS, patches, count), jnp.float32),
            pltpu.VMEM((width, count), jnp.float32),
            pltpu.VMEM((apart[0], sizes[1], *apart[1:]), jnp.bfloat16),
            pltpu.VMEM(lines, jnp.float32),
            pltpu.VMEM(lines, jnp.float32),
            pltpu.VMEM(pairs.shape, pairs.dtype),
            pltpu.SemaphoreType.DMA(()),
            pltpu.SemaphoreType.DMA((2,)),
        ],
        compiler_params=pltpu.CompilerParams(vmem_limit_bytes=VMEM_BYTES),
        cost_estimate=pl.CostEstimate(
            flops=6 * flops, bytes_accessed=3 << 20, transcendentals=HEADS * patches * count
        ),
        name="pairs",
    )(pltpu.with_memory_space_constraint(pairs, pltpu.HBM), all_text, keys[0], values[0])
    return own, other, second, grad_keys.reshape(keys.shape), grad_values.reshape(values.shape)


def local(text, keys, values, pair_image):
    width = text.shape[1]
    image_total = lax.axis_size(OVER)
    all_text = gathered(text)
    own, other, second, grad_keys, grad_values = one_image(
        tuple(lax.axis_size(axis) for axis in OVER),
        pair_image.reshape(1, -1),
        all_text,
        keys,
        values,
    )
    loss, grad_text = summed(own, other, second, image_total, width)
    return (loss.reshape(1), grad_text, grad_keys, grad_values)


def solution(mesh):
    torus = Mesh(mesh.devices.reshape(2, 2, 2, 4, 16), OVER)
    in_specs = (P(OVER, None), P(OVER, None, None), P(OVER, None, None), P())
    out_specs = (P(OVER), P(OVER, None), P(OVER, None, None), P(OVER, None, None))
    return jax.shard_map(local, mesh=torus, in_specs=in_specs, out_specs=out_specs, check_vma=False)
```

```python
import functools

import jax
import jax.numpy as jnp
from jax import lax
from jax.experimental import pallas as pl
from jax.experimental.pallas import tpu as pltpu
from jax.sharding import Mesh
from jax.sharding import PartitionSpec as P

HEADS = 8
OVER = ("x_lo", "core", "x_hi", "y", "z")
PLANE = ("x_lo", "x_hi", "y")
LINE = ("core", "z")


EPS = 1e-06
LOGIT_SCALE = 10.0
LOGIT_BIAS = -1.0
LANES = 128
LOSS_LANES = 128
VMEM_BYTES = 24 << 20
SMALL_BYTES = 4 << 20


def exchanged(parts, axes):
    return lax.all_to_all(parts, axes, 0, 0, tiled=True)


def copies_kernel(row_ref, copies_ref):
    count, blocks, lanes = copies_ref.shape
    row = row_ref[...].astype(jnp.float32)
    cut = [row[:, lanes * block : lanes * (block + 1)] for block in range(blocks)]
    cut = jnp.concatenate(cut, axis=0).astype(jnp.bfloat16)
    copies_ref[...] = jnp.broadcast_to(cut[None], copies_ref.shape)


def rows_kernel(cut_ref, copies_ref):
    cut = cut_ref[...].astype(jnp.float32)
    rows = [cut[:, block] for block in range(cut.shape[1])]
    rows = jnp.concatenate(rows, axis=1).astype(jnp.bfloat16)
    copies_ref[...] = jnp.broadcast_to(rows[None], copies_ref.shape)


def total_kernel(image_total, parts_ref, loss_ref, grad_ref):
    width = grad_ref.shape[1]
    total = jnp.sum(parts_ref[...], axis=0)
    grad_ref[...] = total[:, :width]
    loss_ref[...] = total[:, width : width + 1] * (1.0 / image_total)


def gathered(row):
    width = row.shape[1]
    line, plane = lax.axis_size(LINE), lax.axis_size(PLANE)
    inside = pl.BlockSpec(memory_space=pltpu.VMEM)
    copies = pl.pallas_call(
        copies_kernel,
        out_shape=jax.ShapeDtypeStruct((line, width // LANES, LANES), row.dtype),
        in_specs=[inside],
        out_specs=inside,
        compiler_params=pltpu.CompilerParams(vmem_limit_bytes=SMALL_BYTES),
        name="copies",
    )(row)
    rows = pl.pallas_call(
        rows_kernel,
        out_shape=jax.ShapeDtypeStruct((plane, line, width), row.dtype),
        in_specs=[inside],
        out_specs=inside,
        compiler_params=pltpu.CompilerParams(vmem_limit_bytes=SMALL_BYTES),
        name="rows",
    )(exchanged(copies, LINE))
    return exchanged(rows, PLANE).reshape(-1, width)


def summed(own, other, second, image_total, width):
    both = lax.all_gather(other, LINE[0], axis=0)
    swapped = jnp.where(second > 0, both[0], both[1])
    parts = (own.astype(jnp.float32) + swapped.astype(jnp.float32)).astype(own.dtype)
    parts = jnp.sum(exchanged(parts, PLANE).astype(jnp.float32), axis=0)
    parts = exchanged(parts[:, None], LINE[1:])
    inside = pl.BlockSpec(memory_space=pltpu.VMEM)
    return pl.pallas_call(
        functools.partial(total_kernel, image_total),
        out_shape=(
            jax.ShapeDtypeStruct((1, 1), jnp.float32),
            jax.ShapeDtypeStruct((1, width), jnp.float32),
        ),
        in_specs=[inside],
        out_specs=(inside, inside),
        compiler_params=pltpu.CompilerParams(vmem_limit_bytes=SMALL_BYTES),
        name="total",
    )(parts)


def gathered_place(caption, sizes):
    index = {}
    for axis, size in reversed(tuple(zip(OVER, sizes))):
        index[axis] = lax.rem(caption, size)
        caption = lax.div(caption, size)
    place = jnp.zeros_like(caption)
    for axis in PLANE + LINE:
        place = place * sizes[OVER.index(axis)] + index[axis]
    return place


def padded_head(rows, head):
    zeros = jnp.zeros_like(rows)
    return jnp.concatenate([rows, zeros] if head % 2 == 0 else [zeros, rows], axis=0)


def pair_kernel(
    sizes, pairs_ref, text_ref, keys_ref, values_ref,
    own_ref, other_ref, second_ref, grad_keys, grad_values,
    keys_t, values_t, text_t, dout_t, attn, dscore, weights, pooled, sums,
    pairs_in, arrived,
):
    pairs_copy = pltpu.make_async_copy(pairs_ref, pairs_in, arrived)
    pairs_copy.start()
    count, width = text_ref.shape
    patches = keys_ref.shape[0]
    depth = width // HEADS
    scale = depth ** (-0.5)
    blocks = HEADS // 2
    text_square = pool_square = pool_text = jnp.zeros((1, count), jnp.float32)
    def rows_of(head):
        return slice(head * depth, (head + 1) * depth)

    def lanes_of(head):
        return slice(head // 2 * 2 * depth, (head // 2 + 1) * 2 * depth)

    def scored(head):
        lanes = lanes_of(head)
        if head % 2 == 0:
            text_t[lanes, :] = text_ref[:, lanes].T
            values_t[lanes, :] = values_ref[:, lanes].T
        query = text_t[rows_of(head), :]
        return jnp.dot(
            keys_ref[:, lanes],
            padded_head(query * jnp.asarray(scale, query.dtype), head),
            preferred_element_type=jnp.float32,
        )

    scores = [scored(head) for head in range(HEADS)]
    for head in range(HEADS + 1):
        if head > 0:
            rows = rows_of(head - 1)
            pool = jnp.dot(values_t[rows, :], attn[head - 1], preferred_element_type=jnp.float32)
            pooled[rows, :] = pool
            wide = text_t[rows, :].astype(jnp.float32)
            text_square += jnp.sum(wide * wide, 0, keepdims=True)
            pool_square += jnp.sum(pool * pool, 0, keepdims=True)
            pool_text += jnp.sum(pool * wide, 0, keepdims=True)
        if head < HEADS:
            grown = jnp.exp(scores[head] - jnp.max(scores[head], 0, keepdims=True))
            weight = grown * (1.0 / jnp.sum(grown, 0, keepdims=True))
            weights[head] = weight
            attn[head] = weight.astype(jnp.bfloat16)
    tnorm = lax.rsqrt(text_square * (1.0 / width) + EPS)
    pnorm = lax.rsqrt(pool_square * (1.0 / width) + EPS)
    cosine = pool_text * (1.0 / width) * pnorm * tnorm
    logit = LOGIT_SCALE * cosine + LOGIT_BIAS
    captions = lax.broadcasted_iota(jnp.int32, (1, count), 1)
    pairs_copy.wait()
    described = jnp.where(pairs_in[...] == lax.axis_index(OVER), captions, 0)
    matching = gathered_place(jnp.sum(described, 1, keepdims=True), sizes)
    label = jnp.where(captions == matching, 1.0, -1.0).astype(jnp.float32)
    margin = -label * logit
    loss = jnp.maximum(margin, 0.0) + jnp.log1p(jnp.exp(-jnp.abs(margin)))
    slope = -label / (1.0 + jnp.exp(-margin))
    dcos = LOGIT_SCALE / width * slope
    out_text, out_pool = pnorm * dcos * tnorm, pnorm * dcos * cosine * pnorm
    direct_pool, direct_text = tnorm * dcos * pnorm, tnorm * dcos * cosine * tnorm

    def over_captions(parts, rows_t, head):
        return lax.dot_general(
            parts[head],
            padded_head(rows_t[head * depth : (head + 1) * depth, :], head),
            (((1,), (1,)), ((), ())),
            preferred_element_type=jnp.float32,
        )

    parts = (sizes[0] * sizes[2] * sizes[3], sizes[1], sizes[4])
    def attended(head):
        lanes, rows = lanes_of(head), rows_of(head)
        if head % 2 == 0:
            keys_t[lanes, :] = keys_ref[:, lanes].T
        wide = text_t[rows, :].astype(jnp.float32)
        pool = pooled[rows, :]
        dout = (out_text * wide - out_pool * pool).astype(jnp.bfloat16)
        dout_t[rows, :] = dout
        pooled[rows, :] = direct_pool * pool - direct_text * wide
        return jnp.dot(
            values_ref[:, lanes], padded_head(dout, head), preferred_element_type=jnp.float32
        )

    dattn = [attended(head) for head in range(HEADS)]
    for head in range(HEADS + 1):
        if head > 0:
            rows = rows_of(head - 1)
            pooled[rows, :] += jnp.dot(
                keys_t[rows, :], dscore[head - 1], preferred_element_type=jnp.float32
            )
        if head > 0 and head % 2 == 0:
            block = head // 2 - 1
            lanes = lanes_of(head - 1)
            sums[..., lanes] = pooled[lanes, :].T.astype(jnp.bfloat16).reshape(*parts, 2 * depth)
            lines = pl.ds(block, patches, stride=blocks)
            grad_values[lines, :] = over_captions(attn, dout_t, 2 * block) + over_captions(
                attn, dout_t, 2 * block + 1
            )
            first = lax.broadcasted_iota(jnp.int32, (1, 2 * depth), 1) < depth
            near, far = (
                jnp.dot(
                    dscore[2 * block + k], text_ref[:, lanes], preferred_element_type=jnp.float32
                )
                for k in range(2)
            )
            grad_keys[lines, :] = jnp.where(first, near, far)
        if head < HEADS:
            weight = weights[head]
            carried = jnp.sum(weight * dattn[head], 0, keepdims=True)
            dscore[head] = (weight * scale * (dattn[head] - carried)).astype(jnp.bfloat16)
    losses = jnp.broadcast_to(loss, (LOSS_LANES, count)).T.astype(jnp.bfloat16)
    sums[..., width:] = losses.reshape(*parts, LOSS_LANES)
    core = lax.axis_index(LINE[0])
    own_ref[...] = sums[:, core]
    other_ref[...] = sums[:, 1 - core]
    second_ref[...] = jnp.full(second_ref.shape, core, jnp.float32)


def one_image(sizes, pairs, all_text, keys, values):
    patches, width = keys.shape[1:]
    count = all_text.shape[0]
    flops = 2 * count * patches * width
    lines = (patches * HEADS // 2, 2 * width // HEADS)
    apart = (sizes[0] * sizes[2] * sizes[3], sizes[4], width + LOSS_LANES)
    inside = pl.BlockSpec(memory_space=pltpu.VMEM)
    anywhere = pl.BlockSpec(memory_space=pl.ANY)
    tall_text = pltpu.VMEM((width, count), jnp.bfloat16)
    tall_image = pltpu.VMEM((width, patches), jnp.bfloat16)
    per_head = pltpu.VMEM((HEADS, patches, count), jnp.bfloat16)
    own, other, second, grad_keys, grad_values = pl.pallas_call(
        functools.partial(pair_kernel, sizes),
        out_shape=(
            jax.ShapeDtypeStruct(apart, jnp.bfloat16),
            jax.ShapeDtypeStruct(apart, jnp.bfloat16),
            jax.ShapeDtypeStruct((1, apart[2]), jnp.float32),
            jax.ShapeDtypeStruct(lines, jnp.float32),
            jax.ShapeDtypeStruct(lines, jnp.float32),
        ),
        in_specs=[
            anywhere,
            *[inside] * 3,
        ],
        out_specs=(inside,) * 5,
        scratch_shapes=[
            tall_image,
            tall_image,
            tall_text,
            tall_text,
            per_head,
            per_head,
            pltpu.VMEM((HEADS, patches, count), jnp.float32),
            pltpu.VMEM((width, count), jnp.float32),
            pltpu.VMEM((apart[0], sizes[1], *apart[1:]), jnp.bfloat16),
            pltpu.VMEM(pairs.shape, pairs.dtype),
            pltpu.SemaphoreType.DMA(()),
        ],
        compiler_params=pltpu.CompilerParams(vmem_limit_bytes=VMEM_BYTES),
        cost_estimate=pl.CostEstimate(
            flops=6 * flops, bytes_accessed=3 << 20, transcendentals=HEADS * patches * count
        ),
        name="pairs",
    )(pltpu.with_memory_space_constraint(pairs, pltpu.HBM), all_text, keys[0], values[0])
    return own, other, second, grad_keys.reshape(keys.shape), grad_values.reshape(values.shape)


def local(text, keys, values, pair_image):
    width = text.shape[1]
    image_total = lax.axis_size(OVER)
    all_text = gathered(text)
    own, other, second, grad_keys, grad_values = one_image(
        tuple(lax.axis_size(axis) for axis in OVER),
        pair_image.reshape(1, -1),
        all_text,
        keys,
        values,
    )
    loss, grad_text = summed(own, other, second, image_total, width)
    return (loss.reshape(1), grad_text, grad_keys, grad_values)


def solution(mesh):
    torus = Mesh(mesh.devices.reshape(2, 2, 2, 4, 16), OVER)
    in_specs = (P(OVER, None), P(OVER, None, None), P(OVER, None, None), P())
    out_specs = (P(OVER), P(OVER, None), P(OVER, None, None), P(OVER, None, None))
    return jax.shard_map(local, mesh=torus, in_specs=in_specs, out_specs=out_specs, check_vma=False)
```
